32 devices in a mesh: bins: 8 (over z, x), lat: 4 (over y, core).
Axes of the slice: x: 2, y: 2, z: 4, core: 2. Of those that a mesh axis runs over, the one named last changes fastest.
Arguments:
- spectrum: float32 [1152, 64, 384], P('bins', 'lat'), may hold values from 0.05 to 2
- sea_mask: int32 [64, 384], P('lat'), may hold values 0 or 1
- current: float32 [768, 128], P('bins', 'lat'), may hold values from -0.6 to 0.6
- partner_plus: int32 [1152], replicated, may hold values from 0 to 1151
- partner_minus: int32 [1152], replicated, may hold values from 0 to 1151
- source_map: int32 [768, 128], P('bins', 'lat'), may hold values from 0 to 8
Outputs:
- spectrum_out: float32 [1152, 64, 384], P('bins', 'lat')
- stokes: float32 [2, 64, 768, 128], P(None, None, 'bins', 'lat')
The draws below stay inside these ranges and needn't reach their ends.
All inputs are finite; a program needn't handle non-finite values. No bound on the sum of `sea_mask` on one device may be relied on, other than what follows from the above.
Results may differ from the reference program's by a relative error of at most 0.000086.
Values sent between devices are 32-bit elements; how exact they have to be, the bound alone decides.
A program may use at most 128 MiB of HBM per device.

```python
import math
import jax
import jax.numpy as jnp
from jax import lax

NDIR = 36
NFREQ = 32
LEV = 64
NLON = 384
BINS = 1152
NLAT = 64


def with_ends(values, key, low, top_value):
    extent = values.shape
    index_at = [jax.random.randint(jax.random.fold_in(key, axis), (), 0, extent[axis]) for axis in range(len(extent))]
    values = values.at[tuple(index_at)].set(low)
    longest = extent.index(max(extent))
    index_at[longest] = (index_at[longest] + 1) % extent[longest]
    return values.at[tuple(index_at)].set(top_value)


def block_levels(key, shape, split, low, high):
    gain = 1.0
    for axis_at, shards_of in split:
        heights = jax.random.uniform(jax.random.fold_in(jax.random.fold_in(key, 6), axis_at), (shards_of,), jnp.float32, low / len(split), high / len(split))
        gain = gain * jnp.repeat(jnp.exp(heights), shape[axis_at] // shards_of).reshape((-1,) + (1,) * (len(shape) - 1 - axis_at))
    return gain


def gaussian(key, dims, deviation, limit, cuts=(), held_as=jnp.bfloat16):
    values = deviation * jax.random.normal(key, dims, jnp.float32)
    if cuts:
        values = values * block_levels(key, dims, cuts, -0.22, 0.18)
    return jnp.clip(values, -limit, limit).astype(held_as)


def setup_inputs(seed: int = 0) -> dict:
    keys = jax.random.split(jax.random.key(seed), 7)
    return {
        "spectrum": jnp.clip(jnp.exp(math.log(2.0) - 3.6888794 * jax.random.uniform(keys[0], (BINS, NLAT, NLON), jnp.float32) ** block_levels(keys[0], (BINS, NLAT, NLON), ((0, 8), (1, 4)), -0.2, 0.2)), 0.05, 2.0),
        "sea_mask": with_ends((jax.random.randint(keys[1], (NLAT, NLON), 0, 5) < 4).astype(jnp.int32), jax.random.fold_in(keys[1], 1), 0, 1),
        "current": gaussian(keys[2], (2 * NLON, 2 * NLAT), 0.15, 0.6, ((0, 8), (1, 4)), jnp.float32),
        "partner_plus": with_ends(jax.random.randint(keys[3], (BINS,), 0, BINS), jax.random.fold_in(keys[3], 1), 0, BINS - 1).astype(jnp.int32),
        "partner_minus": with_ends(jax.random.randint(keys[4], (BINS,), 0, BINS), jax.random.fold_in(keys[4], 1), 0, BINS - 1).astype(jnp.int32),
        "source_map": with_ends(jax.random.randint(keys[5], (2 * NLON, 2 * NLAT), 0, 9), jax.random.fold_in(keys[5], 1), 0, 8).astype(jnp.int32),
    }


HIGHEST = lax.Precision.HIGHEST

def bin_tables():
    dir_index = jnp.arange(NDIR, dtype=jnp.float32)
    freq_index = jnp.arange(NFREQ, dtype=jnp.float32)
    angles = 2.0 * math.pi * (dir_index + 0.5) / NDIR
    speeds = 0.12 + 0.25 * (NFREQ - 1 - freq_index) / (NFREQ - 1)
    along_x = jnp.repeat(speeds, NDIR) * jnp.tile(jnp.cos(angles), NFREQ)
    along_y = jnp.repeat(speeds, NDIR) * jnp.tile(jnp.sin(angles), NFREQ)
    strength = jnp.repeat(0.06 * (1.0 + freq_index / (NFREQ - 1)), NDIR)
    levels = jnp.arange(LEV, dtype=jnp.float32) + 0.5
    wavenumber = 0.02 * jnp.power(1.15, freq_index)
    decay = jnp.repeat(jnp.exp(-levels[:, None] * wavenumber[None, :]), NDIR, axis=1)
    amplitude = 2.0 / math.sqrt(NDIR * NFREQ)
    cosines = jnp.tile(jnp.cos(angles), NFREQ)
    sines = jnp.tile(jnp.sin(angles), NFREQ)
    drift_table = amplitude * jnp.concatenate([decay * cosines[None, :], decay * sines[None, :]], axis=0)
    return (along_x, along_y, strength, drift_table)

def cell_means(current_cells):
    lon_count = current_cells.shape[0] // 2
    lat_count = current_cells.shape[1] // 2
    return current_cells.reshape(lon_count, 2, lat_count, 2).mean(axis=(1, 3))

def face_fluxes(padded, velocity, dimension):
    face_count = padded.shape[dimension] - 3

    def section(low_edge):
        return lax.slice_in_dim(padded, low_edge, low_edge + face_count, axis=dimension)
    left_value = (-section(0) + 5.0 * section(1) + 2.0 * section(2)) / 6.0
    right_value = (2.0 * section(1) + 5.0 * section(2) - section(3)) / 6.0
    return jnp.maximum(velocity, 0.0) * left_value + jnp.minimum(velocity, 0.0) * right_value

def transport(padded_rows, zonal_flow, along_x, along_y, sea_cells):
    row_count = padded_rows.shape[1] - 4
    spectra = padded_rows[:, 2:2 + row_count, :]
    padded_cols = jnp.pad(spectra, ((0, 0), (0, 0), (2, 2)))
    zonal_padded = jnp.pad(zonal_flow, ((0, 0), (1, 1)))
    face_zonal = 0.5 * (zonal_padded[:, :-1] + zonal_padded[:, 1:])
    speed_x = along_x[:, None, None] + face_zonal[None, :, :]
    flux_x = face_fluxes(padded_cols, speed_x, 2)
    flux_y = face_fluxes(padded_rows, along_y[:, None, None], 1)
    change = flux_x[:, :, 1:] - flux_x[:, :, :-1] + flux_y[:, 1:, :] - flux_y[:, :-1, :]
    return sea_cells[None, :, :] * (spectra - change)

def transport_all(spectra, zonal_flow, along_x, along_y, sea_cells):
    grouped = spectra.reshape(NFREQ, NDIR, NLAT, NLON)

    def one_bundle(entries):
        bundle, speed_x, speed_y = entries
        padded = jnp.pad(bundle, ((0, 0), (2, 2), (0, 0)))
        return transport(padded, zonal_flow, speed_x, speed_y, sea_cells)
    carried = lax.map(one_bundle, (grouped, along_x.reshape(NFREQ, NDIR), along_y.reshape(NFREQ, NDIR)))
    return carried.reshape(NDIR * NFREQ, NLAT, NLON)

def spread_to_ocean(rim, source_map):
    row_count = rim.shape[1] - 2
    col_count = rim.shape[2] - 2
    result = jnp.zeros((rim.shape[0], 2 * col_count, 2 * row_count), jnp.float32)
    for offset in range(9):
        row_shift = offset // 3 - 1
        col_shift = offset % 3 - 1
        shifted = rim[:, 1 + row_shift:1 + row_shift + row_count, 1 + col_shift:1 + col_shift + col_count]
        shifted = jnp.swapaxes(shifted, 1, 2)
        shifted = jnp.repeat(jnp.repeat(shifted, 2, axis=1), 2, axis=2)
        result = result + jnp.where(source_map[None, :, :] == offset, shifted, jnp.float32(0.0))
    return result

def reference(spectrum, sea_mask, current, partner_plus, partner_minus, source_map):
    along_x, along_y, strength, drift_table = bin_tables()
    sea_cells = sea_mask.astype(jnp.float32)
    zonal_flow = cell_means(current).T
    masked = spectrum * sea_cells[None, :, :]
    after_first = transport_all(masked, zonal_flow, along_x, along_y, sea_cells)
    bin_count = NDIR * NFREQ
    flat_rows = after_first.reshape(bin_count, NLAT * NLON)
    plus_part = jnp.take(flat_rows, partner_plus, axis=0)
    minus_part = jnp.take(flat_rows, partner_minus, axis=0)
    source = strength[:, None] * (flat_rows * flat_rows * (plus_part + minus_part) - 2.0 * flat_rows * plus_part * minus_part)
    back = jax.ops.segment_sum(source, partner_plus, num_segments=bin_count) + jax.ops.segment_sum(source, partner_minus, num_segments=bin_count)
    middle = flat_rows + (source - 0.5 * back)
    drift_rows = jnp.dot(drift_table, middle, precision=HIGHEST).reshape(2 * LEV, NLAT, NLON)
    rim = jnp.pad(drift_rows, ((0, 0), (1, 1), (1, 1)))
    stokes = spread_to_ocean(rim, source_map).reshape(2, LEV, 2 * NLON, 2 * NLAT)
    second = transport_all(middle.reshape(bin_count, NLAT, NLON), zonal_flow, along_x, along_y, sea_cells)
    return (second, stokes)
```

```python
import functools
import math

import jax
import jax.numpy as jnp
from jax import lax
from jax.experimental import pallas as pl
from jax.experimental.pallas import tpu as pltpu
from jax.sharding import PartitionSpec as P

NDIR = 36
NFREQ = 32
LEV = 64


HIGHEST = lax.Precision.HIGHEST


def extended(block, sides, width):
    for axis, dim in sides:
        count = lax.axis_size(axis)
        forward = [(i, i + 1) for i in range(count - 1)]
        backward = [(target, source) for source, target in forward]
        low = lax.ppermute(
            lax.slice_in_dim(block, block.shape[dim] - width, None, axis=dim), axis, forward
        )
        high = lax.ppermute(lax.slice_in_dim(block, 0, width, axis=dim), axis, backward)
        block = jnp.concatenate([low, block, high], axis=dim)
    return block


def bin_tables():
    dir_index = jnp.arange(NDIR, dtype=jnp.float32)
    freq_index = jnp.arange(NFREQ, dtype=jnp.float32)
    angles = 2.0 * math.pi * (dir_index + 0.5) / NDIR
    speeds = 0.12 + 0.25 * (NFREQ - 1 - freq_index) / (NFREQ - 1)
    along_x = jnp.repeat(speeds, NDIR) * jnp.tile(jnp.cos(angles), NFREQ)
    along_y = jnp.repeat(speeds, NDIR) * jnp.tile(jnp.sin(angles), NFREQ)
    strength = jnp.repeat(0.06 * (1.0 + freq_index / (NFREQ - 1)), NDIR)
    levels = jnp.arange(LEV, dtype=jnp.float32) + 0.5
    wavenumber = 0.02 * jnp.power(1.15, freq_index)
    decay = jnp.repeat(jnp.exp(-levels[:, None] * wavenumber[None, :]), NDIR, axis=1)
    amplitude = 2.0 / math.sqrt(NDIR * NFREQ)
    cosines = jnp.tile(jnp.cos(angles), NFREQ)
    sines = jnp.tile(jnp.sin(angles), NFREQ)
    drift_table = amplitude * jnp.concatenate(
        [decay * cosines[None, :], decay * sines[None, :]], axis=0
    )
    return (along_x, along_y, strength, drift_table)


def cell_means(current_cells):
    lon_count = current_cells.shape[0] // 2
    lat_count = current_cells.shape[1] // 2
    return current_cells.reshape(lon_count, 2, lat_count, 2).mean(axis=(1, 3))


def face_fluxes(padded, velocity, dimension):
    face_count = padded.shape[dimension] - 3

    def section(low_edge):
        return lax.slice_in_dim(padded, low_edge, low_edge + face_count, axis=dimension)

    left_value = (-section(0) + 5.0 * section(1) + 2.0 * section(2)) / 6.0
    right_value = (2.0 * section(1) + 5.0 * section(2) - section(3)) / 6.0
    return jnp.maximum(velocity, 0.0) * left_value + jnp.minimum(velocity, 0.0) * right_value


def transport(padded_rows, zonal_flow, along_x, along_y, sea_cells):
    row_count = padded_rows.shape[1] - 4
    spectra = padded_rows[:, 2 : 2 + row_count, :]
    padded_cols = jnp.pad(spectra, ((0, 0), (0, 0), (2, 2)))
    zonal_padded = jnp.pad(zonal_flow, ((0, 0), (1, 1)))
    face_zonal = 0.5 * (zonal_padded[:, :-1] + zonal_padded[:, 1:])
    speed_x = along_x[:, None, None] + face_zonal[None, :, :]
    flux_x = face_fluxes(padded_cols, speed_x, 2)
    flux_y = face_fluxes(padded_rows, along_y[:, None, None], 1)
    change = flux_x[:, :, 1:] - flux_x[:, :, :-1] + flux_y[:, 1:, :] - flux_y[:, :-1, :]
    return sea_cells[None, :, :] * (spectra - change)


def spread_to_ocean(rim, source_map):
    row_count = rim.shape[1] - 2
    col_count = rim.shape[2] - 2
    result = jnp.zeros((rim.shape[0], 2 * col_count, 2 * row_count), jnp.float32)
    for offset in range(9):
        row_shift = offset // 3 - 1
        col_shift = offset % 3 - 1
        shifted = rim[
            :, 1 + row_shift : 1 + row_shift + row_count, 1 + col_shift : 1 + col_shift + col_count
        ]
        shifted = jnp.swapaxes(shifted, 1, 2)
        shifted = jnp.repeat(jnp.repeat(shifted, 2, axis=1), 2, axis=2)
        result = result + jnp.where(source_map[None, :, :] == offset, shifted, jnp.float32(0.0))
    return result


def on_device_plain(spectrum, sea_mask, current, partner_plus, partner_minus, source_map):
    along_x, along_y, strength, drift_table = bin_tables()
    bin_count = NDIR * NFREQ
    local_bins = spectrum.shape[0]
    first_bin = lax.axis_index("bins") * local_bins
    local_x = lax.dynamic_slice_in_dim(along_x, first_bin, local_bins)
    local_y = lax.dynamic_slice_in_dim(along_y, first_bin, local_bins)
    sea_cells = sea_mask.astype(jnp.float32)
    strip_flow = cell_means(current)
    zonal_flow = lax.all_gather(strip_flow, "bins", axis=0, tiled=True).T
    masked = spectrum * sea_cells[None, :, :]
    padded = extended(masked, (("lat", 1),), 2)
    after_first = transport(padded, zonal_flow, local_x, local_y, sea_cells)
    bin_ids = jnp.arange(bin_count, dtype=jnp.int32)
    plus_table = (partner_plus[:, None] == bin_ids[None, :]).astype(jnp.float32)
    minus_table = (partner_minus[:, None] == bin_ids[None, :]).astype(jnp.float32)
    contract_first = (((0,), (0,)), ((), ()))
    arrived = lax.all_to_all(after_first, "bins", split_axis=2, concat_axis=0, tiled=True)
    row_count = arrived.shape[1]
    col_count = arrived.shape[2]
    flat_rows = arrived.reshape(bin_count, row_count * col_count)
    plus_part = jnp.dot(plus_table, flat_rows, precision=HIGHEST)
    minus_part = jnp.dot(minus_table, flat_rows, precision=HIGHEST)
    source = strength[:, None] * (
        flat_rows * flat_rows * (plus_part + minus_part) - 2.0 * flat_rows * plus_part * minus_part
    )
    back = lax.dot_general(plus_table, source, contract_first, precision=HIGHEST) + lax.dot_general(
        minus_table, source, contract_first, precision=HIGHEST
    )
    middle = flat_rows + (source - 0.5 * back)
    drift_rows = jnp.dot(drift_table, middle, precision=HIGHEST)
    middle, drift_rows = (
        middle.reshape(bin_count, row_count, col_count),
        drift_rows.reshape(2 * LEV, row_count, col_count),
    )
    rim = extended(drift_rows, (("bins", 2), ("lat", 1)), 1)
    ocean = spread_to_ocean(rim, source_map)
    stokes = ocean.reshape(2, LEV, ocean.shape[1], ocean.shape[2])
    returned = lax.all_to_all(middle, "bins", split_axis=0, concat_axis=2, tiled=True)
    padded_again = extended(returned, (("lat", 1),), 2)
    second = transport(padded_again, zonal_flow, local_x, local_y, sea_cells)
    return (second, stokes)


MESH = pl.DeviceIdType.MESH
TILE = 128
EDGE = 8
VMEM = pltpu.VMEM


def enter(count, me):
    barrier = pltpu.get_barrier_semaphore()
    for step in range(1, count):
        pl.semaphore_signal(
            barrier,
            inc=1,
            device_id={"bins": lax.rem(me + step, count)},
            device_id_type=MESH,
        )
    pl.semaphore_wait(barrier, count - 1)


def gather_kernel(count, strip_ref, out_ref, send_sem, recv_sem):
    me = lax.axis_index("bins")
    enter(count, me)
    copies = []
    for step in range(1, count):
        copy = pltpu.make_async_remote_copy(
            src_ref=strip_ref,
            dst_ref=out_ref.at[me],
            send_sem=send_sem.at[step],
            recv_sem=recv_sem.at[step],
            device_id={"bins": lax.rem(me + step, count)},
            device_id_type=MESH,
        )
        copy.start()
        copies.append(copy)
    own = pltpu.make_async_copy(strip_ref, out_ref.at[me], send_sem.at[0])
    own.start()
    own.wait()
    for copy in copies:
        copy.wait()


def gather_strips(strip, count):
    return pl.pallas_call(
        functools.partial(gather_kernel, count),
        out_shape=jax.ShapeDtypeStruct((count,) + strip.shape, strip.dtype),
        in_specs=[pl.BlockSpec(memory_space=VMEM)],
        out_specs=pl.BlockSpec(memory_space=VMEM),
        scratch_shapes=[
            pltpu.SemaphoreType.DMA((count,)),
            pltpu.SemaphoreType.DMA((count,)),
        ],
        compiler_params=pltpu.CompilerParams(collective_id=0, has_side_effects=True),
    )(strip)


def transport_kernel(bins_first, x_ref, low_ref, high_ref, mask_ref, half_ref, coef_ref, out_ref):
    rows = mask_ref.shape[0]
    cols = mask_ref.shape[1]
    blocks = coef_ref.shape[0] // 8
    lane = lax.broadcasted_iota(jnp.int32, (8, cols), 1)
    at_first = lane == 0
    at_second = lane <= 1
    at_last = lane == cols - 1
    half = half_ref[...]
    half_low = jnp.where(
        lax.broadcasted_iota(jnp.int32, half.shape, 1) == 0, 0.0, pltpu.roll(half, 1, 1)
    )
    sixth = jnp.float32(1.0 / 6.0)

    def block_step(block, carry):
        at = pl.multiple_of(block * 8, 8)
        here = pl.ds(at, 8)
        mask = mask_ref[...]
        low = [low_ref[0, here, :], low_ref[1, here, :]]
        high = [high_ref[0, here, :], high_ref[1, here, :]]
        if bins_first:
            turned = pltpu.einshape("brl->rbl", x_ref[here, :, :] * mask[None])
            inner = [turned[row] for row in range(rows)]
        else:
            inner = [x_ref[row, here, :] for row in range(rows)]
        f = low + inner + high
        coefs = coef_ref[here, :]
        coef = [jnp.broadcast_to(coefs[:, i : i + 1], (8, cols)) for i in range(6)]
        results = []
        for row in range(rows):
            c = f[row + 2]
            m1 = jnp.where(at_first, 0.0, pltpu.roll(c, 1, 1))
            m2 = jnp.where(at_second, 0.0, pltpu.roll(c, 2, 1))
            p1 = jnp.where(at_last, 0.0, pltpu.roll(c, cols - 1, 1))
            own_half = half[row : row + 1, :]
            speed = coef[0] + (own_half + half_low[row : row + 1, :])
            ahead = speed > 0.0
            part = 3.0 * jnp.where(ahead, m1, c) - jnp.where(ahead, m2, p1)
            flux = (speed * sixth) * (part + 2.0 * (m1 + c))
            end_speed = coef[0] + own_half
            end = (end_speed * sixth) * jnp.where(end_speed > 0.0, 5.0 * c - m1, 2.0 * c)
            upper = jnp.where(at_last, end, pltpu.roll(flux, cols - 1, 1))
            along_y = (
                coef[1] * f[row]
                + coef[2] * f[row + 1]
                + coef[3] * c
                + coef[4] * f[row + 3]
                + coef[5] * f[row + 4]
            )
            results.append(mask[row : row + 1, :] * (c - ((upper - flux) + along_y)))
        if bins_first:
            for row in range(rows):
                out_ref[row, here, :] = results[row]
        else:
            out_ref[here, :, :] = pltpu.einshape("rbl->brl", jnp.stack(results))
        return carry

    lax.fori_loop(0, blocks, block_step, 0)


def transport_call(x, low, high, sea_cells, half, coefs, bins_first):
    rows, cols = sea_cells.shape
    bins = coefs.shape[0]
    group = bins // 3 if bins % 24 == 0 else bins
    by_bin = pl.BlockSpec((group, rows, cols), lambda i: (i, 0, 0))
    by_row = pl.BlockSpec((rows, group, cols), lambda i: (0, i, 0))
    edge = pl.BlockSpec((2, group, cols), lambda i: (0, i, 0))
    full = pl.BlockSpec((rows, cols), lambda i: (0, 0))
    return pl.pallas_call(
        functools.partial(transport_kernel, bins_first),
        grid=(bins // group,),
        out_shape=jax.ShapeDtypeStruct(
            (rows, bins, cols) if bins_first else (bins, rows, cols), jnp.float32
        ),
        in_specs=[
            by_bin if bins_first else by_row,
            edge,
            edge,
            full,
            full,
            pl.BlockSpec((group, 8), lambda i: (i, 0)),
        ],
        out_specs=by_row if bins_first else by_bin,
    )(x, low, high, sea_cells, half, coefs)


def halves(value):
    high = value.astype(jnp.bfloat16)
    return high, (value - high.astype(jnp.float32)).astype(jnp.bfloat16)


def middle_kernel(
    count,
    x_ref,
    plus_col_ref,
    minus_col_ref,
    plus_row_ref,
    minus_row_ref,
    strength_ref,
    drift_ref,
    out_ref,
    near_ref,
    arrived,
    middle,
    plus_table,
    minus_table,
    back_table,
    high,
    low,
    source_high,
    source_low,
    total,
    profile,
    in_send,
    in_recv,
    back_send,
    back_recv,
    near_send,
    near_recv,
):
    me = lax.axis_index("bins")
    enter(count, me)
    each = arrived.shape[0]
    bins = arrived.shape[1]
    cols = arrived.shape[2]
    local = bins // count
    tiles = bins // TILE
    own_cols = cols // count
    mine = pl.ds(pl.multiple_of(me * local, 8), local)

    def send(src, dst, send_sem, recv_sem, peer):
        copy = pltpu.make_async_remote_copy(
            src_ref=src,
            dst_ref=dst,
            send_sem=send_sem,
            recv_sem=recv_sem,
            device_id={"bins": peer},
            device_id_type=MESH,
        )
        copy.start()
        return copy

    incoming = []
    for r in range(each):
        group = []
        for step in range(1, count):
            peer = lax.rem(me + step, count)
            group.append(
                send(
                    x_ref.at[peer * each + r],
                    arrived.at[r, mine, :],
                    in_send.at[r, step],
                    in_recv.at[r, step],
                    peer,
                )
            )
        own = pltpu.make_async_copy(
            x_ref.at[me * each + r], arrived.at[r, mine, :], in_send.at[r, 0]
        )
        own.start()
        group.append(own)
        incoming.append(group)

    def table_step(tile, carry):
        here = pl.ds(pl.multiple_of(tile * TILE, TILE), TILE)
        along = lax.broadcasted_iota(jnp.int32, (TILE, bins), 1)
        down = lax.broadcasted_iota(jnp.int32, (TILE, bins), 0) + tile * TILE
        one = jnp.float32(1.0)
        zero = jnp.float32(0.0)
        plus_table[here, :] = jnp.where(plus_col_ref[here, :] == along, one, zero).astype(
            jnp.bfloat16
        )
        minus_table[here, :] = jnp.where(minus_col_ref[here, :] == along, one, zero).astype(
            jnp.bfloat16
        )
        back_table[here, :] = (
            jnp.where(plus_row_ref[...] == down, one, zero)
            + jnp.where(minus_row_ref[...] == down, one, zero)
        ).astype(jnp.bfloat16)
        return carry

    lax.fori_loop(0, tiles, table_step, 0)
    profile[...] = jnp.zeros_like(profile)

    outgoing = []
    for r in range(each):
        for copy in incoming[r]:
            copy.wait()

        def split_step(tile, carry):
            here = pl.ds(pl.multiple_of(tile * TILE, TILE), TILE)
            high[here, :], low[here, :] = halves(arrived[r, here, :])
            return carry

        lax.fori_loop(0, tiles, split_step, 0)

        def pick(table, here, upper, lower):
            rows = table[here, :]
            return jnp.dot(rows, upper[...], preferred_element_type=jnp.float32) + jnp.dot(
                rows, lower[...], preferred_element_type=jnp.float32
            )

        def source_step(tile, carry):
            here = pl.ds(pl.multiple_of(tile * TILE, TILE), TILE)
            plus = pick(plus_table, here, high, low)
            minus = pick(minus_table, here, high, low)
            own_rows = arrived[r, here, :]
            source = strength_ref[here, :] * (
                own_rows * own_rows * (plus + minus) - 2.0 * own_rows * plus * minus
            )
            source_high[here, :], source_low[here, :] = halves(source)
            middle[r, here, :] = own_rows + source
            return carry

        lax.fori_loop(0, tiles, source_step, 0)
        total[...] = jnp.zeros_like(total)

        def back_step(tile, carry):
            here = pl.ds(pl.multiple_of(tile * TILE, TILE), TILE)
            rows = middle[r, here, :] - 0.5 * pick(back_table, here, source_high, source_low)
            middle[r, here, :] = rows
            total[...] += jnp.dot(
                drift_ref[:, here], rows, precision=HIGHEST, preferred_element_type=jnp.float32
            )
            return carry

        lax.fori_loop(0, tiles, back_step, 0)
        for step in range(1, count):
            peer = lax.rem(me + step, count)
            outgoing.append(
                send(
                    middle.at[r, pl.ds(pl.multiple_of(peer * local, 8), local), :],
                    out_ref.at[me * each + r],
                    back_send.at[r, step],
                    back_recv.at[r, step],
                    peer,
                )
            )
        own = pltpu.make_async_copy(
            middle.at[r, mine, :], out_ref.at[me * each + r], back_send.at[r, 0]
        )
        own.start()
        outgoing.append(own)
        profile[r, pl.ds(EDGE, cols), :] = total[...].T

    width = own_cols + 2 * EDGE
    for step in range(1, count):
        peer = lax.rem(me + step, count)
        outgoing.append(
            send(
                profile.at[:, pl.ds(pl.multiple_of(peer * own_cols, 8), width), :],
                near_ref.at[me],
                near_send.at[step],
                near_recv.at[step],
                peer,
            )
        )
    own = pltpu.make_async_copy(
        profile.at[:, pl.ds(pl.multiple_of(me * own_cols, 8), width), :],
        near_ref.at[me],
        near_send.at[0],
    )
    own.start()
    outgoing.append(own)
    for copy in outgoing:
        copy.wait()


def middle_call(x, partner_plus, partner_minus, strength, drift_table, count):
    rows, local, cols = x.shape
    bins = local * count
    each = rows // count
    profiles = drift_table.shape[0]
    width = cols // count + 2 * EDGE
    vmem = pl.BlockSpec(memory_space=VMEM)
    hbm = pl.BlockSpec(memory_space=pl.ANY)
    return pl.pallas_call(
        functools.partial(middle_kernel, count),
        out_shape=(
            jax.ShapeDtypeStruct(x.shape, jnp.float32),
            jax.ShapeDtypeStruct((count, each, width, profiles), jnp.float32),
        ),
        in_specs=[hbm] + [vmem] * 6,
        out_specs=(hbm, hbm),
        scratch_shapes=[
            VMEM((each, bins, cols), jnp.float32),
            VMEM((each, bins, cols), jnp.float32),
            VMEM((bins, bins), jnp.bfloat16),
            VMEM((bins, bins), jnp.bfloat16),
            VMEM((bins, bins), jnp.bfloat16),
            VMEM((bins, cols), jnp.bfloat16),
            VMEM((bins, cols), jnp.bfloat16),
            VMEM((bins, cols), jnp.bfloat16),
            VMEM((bins, cols), jnp.bfloat16),
            VMEM((profiles, cols), jnp.float32),
            VMEM((each, cols + 2 * EDGE, profiles), jnp.float32),
            pltpu.SemaphoreType.DMA((each, count)),
            pltpu.SemaphoreType.DMA((each, count)),
            pltpu.SemaphoreType.DMA((each, count)),
            pltpu.SemaphoreType.DMA((each, count)),
            pltpu.SemaphoreType.DMA((count,)),
            pltpu.SemaphoreType.DMA((count,)),
        ],
        compiler_params=pltpu.CompilerParams(
            collective_id=1, has_side_effects=True, vmem_limit_bytes=56 * 1024 * 1024
        ),
    )(
        x,
        partner_plus[:, None],
        partner_minus[:, None],
        partner_plus[None, :],
        partner_minus[None, :],
        strength[:, None],
        drift_table,
    )


def spread_kernel(depth, near_ref, index_ref, out_ref):
    pairs = index_ref.shape[0]
    for pair in range(pairs):
        rows = near_ref[pl.ds(pair * 2 * depth, 4 * depth), :]
        chosen = lax.broadcasted_iota(jnp.int32, (4 * depth, TILE), 0) == index_ref[pair : pair + 1, :]
        out_ref[:, pl.ds(pair * TILE, TILE)] = lax.dot_general(
            rows,
            jnp.where(chosen, jnp.float32(1.0), jnp.float32(0.0)),
            (((0,), (0,)), ((), ())),
            precision=HIGHEST,
            preferred_element_type=jnp.float32,
        )


def spread_call(near, source_map):
    lons, lats = source_map.shape
    cols, depth, profiles = near.shape
    lon = jnp.arange(lons, dtype=jnp.int32)[:, None]
    lat = jnp.arange(lats, dtype=jnp.int32)[None, :]
    index = (lon // 2 % 2 + source_map % 3) * depth + lat // 2 + source_map // 3 + 1
    return pl.pallas_call(
        functools.partial(spread_kernel, depth),
        out_shape=jax.ShapeDtypeStruct((profiles, lons * lats), jnp.float32),
    )(near.reshape(cols * depth, profiles), index.reshape(lons * lats // TILE, TILE))


def exchange_rows(low_side, high_side):
    count = lax.axis_size("lat")
    forward = [(i, i + 1) for i in range(count - 1)]
    backward = [(target, source) for source, target in forward]
    return lax.ppermute(high_side, "lat", forward), lax.ppermute(low_side, "lat", backward)


def on_device_fast(spectrum, sea_mask, current, partner_plus, partner_minus, source_map):
    count = lax.axis_size("bins")
    along_x, along_y, strength, drift_table = bin_tables()
    local_bins, row_count, col_count = spectrum.shape
    forth = jnp.maximum(along_y, 0.0) / 6.0
    back = jnp.minimum(along_y, 0.0) / 6.0
    zeros = jnp.zeros_like(forth)
    coefs = jnp.stack(
        [
            along_x,
            forth,
            -6.0 * forth - 2.0 * back,
            3.0 * forth - 3.0 * back,
            2.0 * forth + 6.0 * back,
            -back,
            zeros,
            zeros,
        ],
        axis=1,
    )
    coefs = lax.dynamic_slice_in_dim(coefs, lax.axis_index("bins") * local_bins, local_bins)
    sea_cells = sea_mask.astype(jnp.float32)
    strip = 0.5 * cell_means(current).T
    strip_cols = strip.shape[1]
    low_side = jnp.swapaxes(spectrum[:, :2, :] * sea_cells[None, :2, :], 0, 1)
    high_side = jnp.swapaxes(spectrum[:, -2:, :] * sea_cells[None, -2:, :], 0, 1)
    low, high = exchange_rows(low_side, high_side)
    strips = gather_strips(jnp.pad(strip, ((0, 0), (0, TILE - strip_cols))), count)
    half = jnp.swapaxes(strips[:, :, :strip_cols], 0, 1).reshape(row_count, col_count)
    first = transport_call(spectrum, low, high, sea_cells, half, coefs, True)
    middle, near = middle_call(first, partner_plus, partner_minus, strength, drift_table, count)
    low, high = exchange_rows(middle[:2], middle[-2:])
    each, width = near.shape[1:3]
    near = near.reshape(row_count, width, 2 * LEV)[:, EDGE - 1 : width - EDGE + 1]
    below, above = exchange_rows(near[:2], near[-2:])
    near = jnp.concatenate([below, near, above, jnp.zeros_like(near[:4])], axis=0)
    stokes = spread_call(jnp.swapaxes(near, 0, 1), source_map)
    second = transport_call(middle, low, high, sea_cells, half, coefs, False)
    return (second, stokes.reshape(2, LEV, *source_map.shape))


def on_device(spectrum, sea_mask, current, partner_plus, partner_minus, source_map):
    count = lax.axis_size("bins")
    bins, rows, cols = spectrum.shape
    lons, lats = source_map.shape
    fits = (
        rows % count == 0
        and rows % 8 == 0
        and bins % 8 == 0
        and cols % TILE == 0
        and cols // count % 8 == 0
        and cols // count <= TILE
        and bins * count % TILE == 0
        and 4 * lats == TILE
        and lons % 4 == 0
    )
    body = on_device_fast if fits else on_device_plain
    return body(spectrum, sea_mask, current, partner_plus, partner_minus, source_map)


def solution(mesh):
    return jax.shard_map(
        on_device,
        mesh=mesh,
        in_specs=(
            P("bins", "lat", None),
            P("lat", None),
            P("bins", "lat"),
            P(),
            P(),
            P("bins", "lat"),
        ),
        out_specs=(P("bins", "lat", None), P(None, None, "bins", "lat")),
        check_vma=False,
    )
```

```python
import functools
import math

import jax
import jax.numpy as jnp
import numpy as np
from jax import lax
from jax.experimental import pallas as pl
from jax.experimental.pallas import tpu as pltpu
from jax.sharding import PartitionSpec as P

NDIR = 36
NFREQ = 32
LEV = 64


HIGHEST = lax.Precision.HIGHEST


def extended(block, sides, width):
    for axis, dim in sides:
        count = lax.axis_size(axis)
        forward = [(i, i + 1) for i in range(count - 1)]
        backward = [(target, source) for source, target in forward]
        low = lax.ppermute(
            lax.slice_in_dim(block, block.shape[dim] - width, None, axis=dim), axis, forward
        )
        high = lax.ppermute(lax.slice_in_dim(block, 0, width, axis=dim), axis, backward)
        block = jnp.concatenate([low, block, high], axis=dim)
    return block


def bin_tables():
    dir_index = jnp.arange(NDIR, dtype=jnp.float32)
    freq_index = jnp.arange(NFREQ, dtype=jnp.float32)
    angles = 2.0 * math.pi * (dir_index + 0.5) / NDIR
    speeds = 0.12 + 0.25 * (NFREQ - 1 - freq_index) / (NFREQ - 1)
    along_x = jnp.repeat(speeds, NDIR) * jnp.tile(jnp.cos(angles), NFREQ)
    along_y = jnp.repeat(speeds, NDIR) * jnp.tile(jnp.sin(angles), NFREQ)
    strength = jnp.repeat(0.06 * (1.0 + freq_index / (NFREQ - 1)), NDIR)
    levels = jnp.arange(LEV, dtype=jnp.float32) + 0.5
    wavenumber = 0.02 * jnp.power(1.15, freq_index)
    decay = jnp.repeat(jnp.exp(-levels[:, None] * wavenumber[None, :]), NDIR, axis=1)
    amplitude = 2.0 / math.sqrt(NDIR * NFREQ)
    cosines = jnp.tile(jnp.cos(angles), NFREQ)
    sines = jnp.tile(jnp.sin(angles), NFREQ)
    drift_table = amplitude * jnp.concatenate(
        [decay * cosines[None, :], decay * sines[None, :]], axis=0
    )
    return (along_x, along_y, strength, drift_table)


def fixed_tables():
    dir_index = np.arange(NDIR, dtype=np.float32)
    freq_index = np.arange(NFREQ, dtype=np.float32)
    angles = 2.0 * math.pi * (dir_index + 0.5) / NDIR
    speeds = 0.12 + 0.25 * (NFREQ - 1 - freq_index) / (NFREQ - 1)
    along_x = np.repeat(speeds, NDIR) * np.tile(np.cos(angles), NFREQ)
    along_y = np.repeat(speeds, NDIR) * np.tile(np.sin(angles), NFREQ)
    strength = np.repeat(0.06 * (1.0 + freq_index / (NFREQ - 1)), NDIR)
    levels = np.arange(LEV, dtype=np.float32) + 0.5
    wavenumber = 0.02 * np.power(np.float32(1.15), freq_index)
    decay = np.repeat(np.exp(-levels[:, None] * wavenumber[None, :]), NDIR, axis=1)
    amplitude = 2.0 / math.sqrt(NDIR * NFREQ)
    cosines = np.tile(np.cos(angles), NFREQ)
    sines = np.tile(np.sin(angles), NFREQ)
    drift_table = amplitude * np.concatenate(
        [decay * cosines[None, :], decay * sines[None, :]], axis=0
    )
    tables = (along_x, along_y, strength, drift_table)
    return tuple(np.asarray(table, dtype=np.float32) for table in tables)


def cell_means(current_cells):
    lon_count = current_cells.shape[0] // 2
    lat_count = current_cells.shape[1] // 2
    return current_cells.reshape(lon_count, 2, lat_count, 2).mean(axis=(1, 3))


def face_fluxes(padded, velocity, dimension):
    face_count = padded.shape[dimension] - 3

    def section(low_edge):
        return lax.slice_in_dim(padded, low_edge, low_edge + face_count, axis=dimension)

    left_value = (-section(0) + 5.0 * section(1) + 2.0 * section(2)) / 6.0
    right_value = (2.0 * section(1) + 5.0 * section(2) - section(3)) / 6.0
    return jnp.maximum(velocity, 0.0) * left_value + jnp.minimum(velocity, 0.0) * right_value


def transport(padded_rows, zonal_flow, along_x, along_y, sea_cells):
    row_count = padded_rows.shape[1] - 4
    spectra = padded_rows[:, 2 : 2 + row_count, :]
    padded_cols = jnp.pad(spectra, ((0, 0), (0, 0), (2, 2)))
    zonal_padded = jnp.pad(zonal_flow, ((0, 0), (1, 1)))
    face_zonal = 0.5 * (zonal_padded[:, :-1] + zonal_padded[:, 1:])
    speed_x = along_x[:, None, None] + face_zonal[None, :, :]
    flux_x = face_fluxes(padded_cols, speed_x, 2)
    flux_y = face_fluxes(padded_rows, along_y[:, None, None], 1)
    change = flux_x[:, :, 1:] - flux_x[:, :, :-1] + flux_y[:, 1:, :] - flux_y[:, :-1, :]
    return sea_cells[None, :, :] * (spectra - change)


def spread_to_ocean(rim, source_map):
    row_count = rim.shape[1] - 2
    col_count = rim.shape[2] - 2
    result = jnp.zeros((rim.shape[0], 2 * col_count, 2 * row_count), jnp.float32)
    for offset in range(9):
        row_shift = offset // 3 - 1
        col_shift = offset % 3 - 1
        shifted = rim[
            :, 1 + row_shift : 1 + row_shift + row_count, 1 + col_shift : 1 + col_shift + col_count
        ]
        shifted = jnp.swapaxes(shifted, 1, 2)
        shifted = jnp.repeat(jnp.repeat(shifted, 2, axis=1), 2, axis=2)
        result = result + jnp.where(source_map[None, :, :] == offset, shifted, jnp.float32(0.0))
    return result


def on_device_plain(spectrum, sea_mask, current, partner_plus, partner_minus, source_map):
    along_x, along_y, strength, drift_table = bin_tables()
    bin_count = NDIR * NFREQ
    local_bins = spectrum.shape[0]
    first_bin = lax.axis_index("bins") * local_bins
    local_x = lax.dynamic_slice_in_dim(along_x, first_bin, local_bins)
    local_y = lax.dynamic_slice_in_dim(along_y, first_bin, local_bins)
    sea_cells = sea_mask.astype(jnp.float32)
    strip_flow = cell_means(current)
    zonal_flow = lax.all_gather(strip_flow, "bins", axis=0, tiled=True).T
    masked = spectrum * sea_cells[None, :, :]
    padded = extended(masked, (("lat", 1),), 2)
    after_first = transport(padded, zonal_flow, local_x, local_y, sea_cells)
    bin_ids = jnp.arange(bin_count, dtype=jnp.int32)
    plus_table = (partner_plus[:, None] == bin_ids[None, :]).astype(jnp.float32)
    minus_table = (partner_minus[:, None] == bin_ids[None, :]).astype(jnp.float32)
    contract_first = (((0,), (0,)), ((), ()))
    arrived = lax.all_to_all(after_first, "bins", split_axis=2, concat_axis=0, tiled=True)
    row_count = arrived.shape[1]
    col_count = arrived.shape[2]
    flat_rows = arrived.reshape(bin_count, row_count * col_count)
    plus_part = jnp.dot(plus_table, flat_rows, precision=HIGHEST)
    minus_part = jnp.dot(minus_table, flat_rows, precision=HIGHEST)
    source = strength[:, None] * (
        flat_rows * flat_rows * (plus_part + minus_part) - 2.0 * flat_rows * plus_part * minus_part
    )
    back = lax.dot_general(plus_table, source, contract_first, precision=HIGHEST) + lax.dot_general(
        minus_table, source, contract_first, precision=HIGHEST
    )
    middle = flat_rows + (source - 0.5 * back)
    drift_rows = jnp.dot(drift_table, middle, precision=HIGHEST)
    middle, drift_rows = (
        middle.reshape(bin_count, row_count, col_count),
        drift_rows.reshape(2 * LEV, row_count, col_count),
    )
    rim = extended(drift_rows, (("bins", 2), ("lat", 1)), 1)
    ocean = spread_to_ocean(rim, source_map)
    stokes = ocean.reshape(2, LEV, ocean.shape[1], ocean.shape[2])
    returned = lax.all_to_all(middle, "bins", split_axis=0, concat_axis=2, tiled=True)
    padded_again = extended(returned, (("lat", 1),), 2)
    second = transport(padded_again, zonal_flow, local_x, local_y, sea_cells)
    return (second, stokes)


MESH = pl.DeviceIdType.MESH
TILE = 128
EDGE = 8
VMEM = pltpu.VMEM


def enter(count, me):
    barrier = pltpu.get_barrier_semaphore()
    for step in range(1, count):
        pl.semaphore_signal(
            barrier,
            inc=1,
            device_id={"bins": lax.rem(me + step, count)},
            device_id_type=MESH,
        )
    pl.semaphore_wait(barrier, count - 1)


def enter_all(count, me, band, bands):
    barrier = pltpu.get_barrier_semaphore()
    for step in range(1, count):
        pl.semaphore_signal(
            barrier,
            inc=1,
            device_id={"bins": lax.rem(me + step, count)},
            device_id_type=MESH,
        )
    for step in (1, bands - 1):
        pl.semaphore_signal(
            barrier,
            inc=1,
            device_id={"lat": lax.rem(band + step, bands)},
            device_id_type=MESH,
        )
    pl.semaphore_wait(barrier, count + 1)


def gather_kernel(count, strip_ref, out_ref, send_sem, recv_sem):
    me = lax.axis_index("bins")
    enter(count, me)
    copies = []
    for step in range(1, count):
        copy = pltpu.make_async_remote_copy(
            src_ref=strip_ref,
            dst_ref=out_ref.at[me],
            send_sem=send_sem.at[step],
            recv_sem=recv_sem.at[step],
            device_id={"bins": lax.rem(me + step, count)},
            device_id_type=MESH,
        )
        copy.start()
        copies.append(copy)
    own = pltpu.make_async_copy(strip_ref, out_ref.at[me], send_sem.at[0])
    own.start()
    own.wait()
    for copy in copies:
        copy.wait()


def gather_strips(strip, count):
    return pl.pallas_call(
        functools.partial(gather_kernel, count),
        out_shape=jax.ShapeDtypeStruct((count,) + strip.shape, strip.dtype),
        in_specs=[pl.BlockSpec(memory_space=VMEM)],
        out_specs=pl.BlockSpec(memory_space=VMEM),
        scratch_shapes=[
            pltpu.SemaphoreType.DMA((count,)),
            pltpu.SemaphoreType.DMA((count,)),
        ],
        compiler_params=pltpu.CompilerParams(collective_id=0, has_side_effects=True),
    )(strip)


def transport_kernel(
    bins_first, x_ref, low_ref, high_ref, mask_ref, half_ref, coef_ref, edge_ref, out_ref
):
    rows = mask_ref.shape[0]
    cols = mask_ref.shape[1]
    blocks = coef_ref.shape[0] // 8
    lane = lax.broadcasted_iota(jnp.int32, (8, cols), 1)
    at_first = lane == 0
    at_second = lane <= 1
    at_last = lane == cols - 1
    half = half_ref[...]
    half_low = jnp.where(
        lax.broadcasted_iota(jnp.int32, half.shape, 1) == 0, 0.0, pltpu.roll(half, 1, 1)
    )
    sixth = jnp.float32(1.0 / 6.0)

    def block_step(block, carry):
        at = pl.multiple_of(block * 8, 8)
        here = pl.ds(at, 8)
        mask = mask_ref[...]
        low = [edge_ref[0:1, :] * low_ref[row, here, :] for row in range(2)]
        high = [edge_ref[1:2, :] * high_ref[row, here, :] for row in range(2)]
        if bins_first:
            turned = pltpu.einshape("brl->rbl", x_ref[here, :, :] * mask[None])
            inner = [turned[row] for row in range(rows)]
        else:
            inner = [x_ref[row, here, :] for row in range(rows)]
        f = low + inner + high
        coefs = coef_ref[here, :]
        coef = [jnp.broadcast_to(coefs[:, i : i + 1], (8, cols)) for i in range(6)]
        results = []
        for row in range(rows):
            c = f[row + 2]
            m1 = jnp.where(at_first, 0.0, pltpu.roll(c, 1, 1))
            m2 = jnp.where(at_second, 0.0, pltpu.roll(c, 2, 1))
            p1 = jnp.where(at_last, 0.0, pltpu.roll(c, cols - 1, 1))
            own_half = half[row : row + 1, :]
            speed = coef[0] + (own_half + half_low[row : row + 1, :])
            ahead = speed > 0.0
            part = 3.0 * jnp.where(ahead, m1, c) - jnp.where(ahead, m2, p1)
            flux = (speed * sixth) * (part + 2.0 * (m1 + c))
            end_speed = coef[0] + own_half
            end = (end_speed * sixth) * jnp.where(end_speed > 0.0, 5.0 * c - m1, 2.0 * c)
            upper = jnp.where(at_last, end, pltpu.roll(flux, cols - 1, 1))
            along_y = (
                coef[1] * f[row]
                + coef[2] * f[row + 1]
                + coef[3] * c
                + coef[4] * f[row + 3]
                + coef[5] * f[row + 4]
            )
            results.append(mask[row : row + 1, :] * (c - ((upper - flux) + along_y)))
        if bins_first:
            for row in range(rows):
                out_ref[row, here, :] = results[row]
        else:
            out_ref[here, :, :] = pltpu.einshape("rbl->brl", jnp.stack(results))
        return carry

    lax.fori_loop(0, blocks, block_step, 0)


def transport_call(x, low, high, sea_cells, half, coefs, edges, bins_first):
    rows, cols = sea_cells.shape
    bins = coefs.shape[0]
    group = bins // 3 if bins % 24 == 0 else bins
    by_bin = pl.BlockSpec((group, rows, cols), lambda i: (i, 0, 0))
    by_row = pl.BlockSpec((rows, group, cols), lambda i: (0, i, 0))
    edge = pl.BlockSpec((2, group, cols), lambda i: (0, i, 0))
    full = pl.BlockSpec((rows, cols), lambda i: (0, 0))
    return pl.pallas_call(
        functools.partial(transport_kernel, bins_first),
        grid=(bins // group,),
        out_shape=jax.ShapeDtypeStruct(
            (rows, bins, cols) if bins_first else (bins, rows, cols), jnp.float32
        ),
        in_specs=[
            by_bin if bins_first else by_row,
            edge,
            edge,
            full,
            full,
            pl.BlockSpec((group, 8), lambda i: (i, 0)),
            pl.BlockSpec((2, cols), lambda i: (0, 0)),
        ],
        out_specs=by_row if bins_first else by_bin,
    )(x, low, high, sea_cells, half, coefs, edges)


def halves(value):
    high = value.astype(jnp.bfloat16)
    return high, (value - high.astype(jnp.float32)).astype(jnp.bfloat16)


def middle_kernel(
    count,
    bands,
    x_ref,
    plus_col_ref,
    minus_col_ref,
    plus_row_ref,
    minus_row_ref,
    strength_ref,
    drift_ref,
    index_ref,
    out_ref,
    low_ref,
    high_ref,
    stokes_ref,
    arrived,
    middle,
    plus_table,
    minus_table,
    back_table,
    high,
    low,
    source_high,
    source_low,
    total,
    profile,
    near,
    ocean,
    in_send,
    in_recv,
    back_send,
    back_recv,
    near_send,
    near_recv,
    edge_send,
    edge_recv,
    ocean_sem,
):
    me = lax.axis_index("bins")
    band = lax.axis_index("lat")
    enter_all(count, me, band, bands)
    each = arrived.shape[0]
    bins = arrived.shape[1]
    cols = arrived.shape[2]
    local = bins // count
    tiles = bins // TILE
    own_cols = cols // count
    mine = pl.ds(pl.multiple_of(me * local, 8), local)

    def send(src, dst, send_sem, recv_sem, peer, axis="bins"):
        copy = pltpu.make_async_remote_copy(
            src_ref=src,
            dst_ref=dst,
            send_sem=send_sem,
            recv_sem=recv_sem,
            device_id={axis: peer},
            device_id_type=MESH,
        )
        copy.start()
        return copy

    incoming = []
    for r in range(each):
        group = []
        for step in range(1, count):
            peer = lax.rem(me + step, count)
            group.append(
                send(
                    x_ref.at[r * count + peer],
                    arrived.at[r, mine, :],
                    in_send.at[r, step],
                    in_recv.at[r, step],
                    peer,
                )
            )
        own = pltpu.make_async_copy(
            x_ref.at[r * count + me], arrived.at[r, mine, :], in_send.at[r, 0]
        )
        own.start()
        group.append(own)
        incoming.append(group)

    def table_step(tile, carry):
        here = pl.ds(pl.multiple_of(tile * TILE, TILE), TILE)
        along = lax.broadcasted_iota(jnp.int32, (TILE, bins), 1)
        down = lax.broadcasted_iota(jnp.int32, (TILE, bins), 0) + tile * TILE
        one = jnp.float32(1.0)
        zero = jnp.float32(0.0)
        plus_table[here, :] = jnp.where(plus_col_ref[here, :] == along, one, zero).astype(
            jnp.bfloat16
        )
        minus_table[here, :] = jnp.where(minus_col_ref[here, :] == along, one, zero).astype(
            jnp.bfloat16
        )
        back_table[here, :] = (
            jnp.where(plus_row_ref[...] == down, one, zero)
            + jnp.where(minus_row_ref[...] == down, one, zero)
        ).astype(jnp.bfloat16)
        return carry

    lax.fori_loop(0, tiles, table_step, 0)
    profile[...] = jnp.zeros_like(profile)

    outgoing = []
    nearby = []
    width = own_cols + 2 * EDGE
    for r in range(each):
        for copy in incoming[r]:
            copy.wait()

        def split_step(tile, carry):
            here = pl.ds(pl.multiple_of(tile * TILE, TILE), TILE)
            high[here, :], low[here, :] = halves(arrived[r, here, :])
            return carry

        lax.fori_loop(0, tiles, split_step, 0)

        def pick(table, here, upper, lower):
            rows = table[here, :]
            return jnp.dot(rows, upper[...], preferred_element_type=jnp.float32) + jnp.dot(
                rows, lower[...], preferred_element_type=jnp.float32
            )

        def source_step(tile, carry):
            here = pl.ds(pl.multiple_of(tile * TILE, TILE), TILE)
            plus = pick(plus_table, here, high, low)
            minus = pick(minus_table, here, high, low)
            own_rows = arrived[r, here, :]
            source = strength_ref[here, :] * (
                own_rows * own_rows * (plus + minus) - 2.0 * own_rows * plus * minus
            )
            source_high[here, :], source_low[here, :] = halves(source)
            middle[r, here, :] = own_rows + source
            return carry

        lax.fori_loop(0, tiles, source_step, 0)
        total[...] = jnp.zeros_like(total)

        def back_step(tile, carry):
            here = pl.ds(pl.multiple_of(tile * TILE, TILE), TILE)
            rows = middle[r, here, :] - 0.5 * pick(back_table, here, source_high, source_low)
            middle[r, here, :] = rows
            total[...] += jnp.dot(
                drift_ref[:, here], rows, precision=HIGHEST, preferred_element_type=jnp.float32
            )
            return carry

        lax.fori_loop(0, tiles, back_step, 0)
        profile[r, pl.ds(EDGE, cols), :] = total[...].T
        for step in range(count):
            peer = lax.rem(me + step, count)
            src = profile.at[r, pl.ds(pl.multiple_of(peer * own_cols, 8), width), :]
            dst = near.at[2 + r * count + me]
            if step == 0:
                copy = pltpu.make_async_copy(src, dst, near_send.at[r, 0])
                copy.start()
            else:
                copy = send(src, dst, near_send.at[r, step], near_recv.at[r, step], peer)
            nearby.append(copy)
        group = []
        for step in range(1, count):
            peer = lax.rem(me + step, count)
            group.append(
                send(
                    middle.at[r, pl.ds(pl.multiple_of(peer * local, 8), local), :],
                    out_ref.at[r * count + me],
                    back_send.at[r, step],
                    back_recv.at[r, step],
                    peer,
                )
            )
        own = pltpu.make_async_copy(
            middle.at[r, mine, :], out_ref.at[r * count + me], back_send.at[r, 0]
        )
        own.start()
        group.append(own)
        outgoing.append(group)

    rows = each * count
    below = lax.rem(band + bands - 1, bands)
    above = lax.rem(band + 1, bands)
    edge_copies = []

    def send_edge(src, dst, slot, peer):
        edge_copies.append(send(src, dst, edge_send.at[slot], edge_recv.at[slot], peer, "lat"))

    for copy in outgoing[0]:
        copy.wait()
    send_edge(out_ref.at[pl.ds(0, 2)], high_ref, 0, below)
    for copy in nearby:
        copy.wait()
    send_edge(near.at[pl.ds(2, 2)], near.at[pl.ds(rows + 2, 2)], 1, below)
    send_edge(near.at[pl.ds(rows, 2)], near.at[pl.ds(0, 2)], 2, above)
    edge_copies[1].wait()
    edge_copies[2].wait()
    near[pl.ds(0, 2)] = near[pl.ds(0, 2)] * jnp.where(band == 0, 0.0, 1.0)
    near[pl.ds(rows + 2, 2)] = near[pl.ds(rows + 2, 2)] * jnp.where(band == bands - 1, 0.0, 1.0)

    ocean_copies = []
    depth = (rows + 4) * 16
    profiles = near.shape[2]
    lats = 2 * rows
    across = TILE // lats
    for octet in range(ocean.shape[1] // 8):
        strips = []
        for pair in range(octet * 8 // across, (octet + 1) * 8 // across):
            base = (EDGE - 1 + pair * across // 2) // 8 * 8
            window = near[:, base : base + 16, :].reshape(depth, profiles)
            chosen = (
                lax.broadcasted_iota(jnp.int32, (depth, TILE), 0) == index_ref[pair : pair + 1, :]
            )
            found = lax.dot_general(
                window,
                jnp.where(chosen, jnp.float32(1.0), jnp.float32(0.0)),
                (((0,), (0,)), ((), ())),
                precision=HIGHEST,
                preferred_element_type=jnp.float32,
            )
            strips += [found[:, i * lats : (i + 1) * lats] for i in range(across)]
        here = pl.ds(octet * 8, 8)
        ocean[:, here, :] = pltpu.einshape("xcl->cxl", jnp.stack(strips))
        copy = pltpu.make_async_copy(
            ocean.at[:, here, :], stokes_ref.at[:, here, :], ocean_sem.at[octet]
        )
        copy.start()
        ocean_copies.append(copy)

    for group in outgoing[1:]:
        for copy in group:
            copy.wait()
    send_edge(out_ref.at[pl.ds(rows - 2, 2)], low_ref, 3, above)
    edge_copies[0].wait()
    edge_copies[3].wait()
    for copy in ocean_copies:
        copy.wait()


def middle_call(x, partner_plus, partner_minus, strength, drift_table, source_map, count, bands):
    rows, local, cols = x.shape
    bins = local * count
    each = rows // count
    profiles = drift_table.shape[0]
    width = cols // count + 2 * EDGE
    lons, lats = source_map.shape
    lon = np.arange(lons, dtype=np.int32)[:, None]
    lat = np.arange(lats, dtype=np.int32)[None, :]
    across = TILE // lats
    base = (EDGE - 1 + lon // across * across // 2) // 8 * 8
    index = (lat // 2 + source_map // 3 + 1) * 16 + (
        EDGE - 1 + lon // 2 - base + source_map % 3
    )
    edge = jax.ShapeDtypeStruct((2, local, cols), jnp.float32)
    vmem = pl.BlockSpec(memory_space=VMEM)
    hbm = pl.BlockSpec(memory_space=pl.ANY)
    return pl.pallas_call(
        functools.partial(middle_kernel, count, bands),
        out_shape=(
            jax.ShapeDtypeStruct(x.shape, jnp.float32),
            edge,
            edge,
            jax.ShapeDtypeStruct((profiles, lons, lats), jnp.float32),
        ),
        in_specs=[hbm] + [vmem] * 7,
        out_specs=(hbm,) * 4,
        scratch_shapes=[
            VMEM((each, bins, cols), jnp.float32),
            VMEM((each, bins, cols), jnp.float32),
            VMEM((bins, bins), jnp.bfloat16),
            VMEM((bins, bins), jnp.bfloat16),
            VMEM((bins, bins), jnp.bfloat16),
            VMEM((bins, cols), jnp.bfloat16),
            VMEM((bins, cols), jnp.bfloat16),
            VMEM((bins, cols), jnp.bfloat16),
            VMEM((bins, cols), jnp.bfloat16),
            VMEM((profiles, cols), jnp.float32),
            VMEM((each, cols + 2 * EDGE, profiles), jnp.float32),
            VMEM((rows + 4, width, profiles), jnp.float32),
            VMEM((profiles, lons, lats), jnp.float32),
            pltpu.SemaphoreType.DMA((each, count)),
            pltpu.SemaphoreType.DMA((each, count)),
            pltpu.SemaphoreType.DMA((each, count)),
            pltpu.SemaphoreType.DMA((each, count)),
            pltpu.SemaphoreType.DMA((each, count)),
            pltpu.SemaphoreType.DMA((each, count)),
            pltpu.SemaphoreType.DMA((4,)),
            pltpu.SemaphoreType.DMA((4,)),
            pltpu.SemaphoreType.DMA((lons // 8,)),
        ],
        compiler_params=pltpu.CompilerParams(
            collective_id=1, has_side_effects=True, vmem_limit_bytes=56 * 1024 * 1024
        ),
    )(
        x,
        partner_plus[:, None],
        partner_minus[:, None],
        partner_plus[None, :],
        partner_minus[None, :],
        strength[:, None],
        drift_table,
        index.reshape(lons * lats // TILE, TILE),
    )


def exchange_rows(low_side, high_side):
    count = lax.axis_size("lat")
    forward = [(i, i + 1) for i in range(count - 1)]
    backward = [(target, source) for source, target in forward]
    return lax.ppermute(high_side, "lat", forward), lax.ppermute(low_side, "lat", backward)


def on_device_fast(spectrum, sea_mask, current, partner_plus, partner_minus, source_map):
    count = lax.axis_size("bins")
    bands = lax.axis_size("lat")
    band = lax.axis_index("lat")
    along_x, along_y, strength, drift_table = fixed_tables()
    local_bins, row_count, col_count = spectrum.shape
    forth = np.maximum(along_y, 0.0) / 6.0
    back = np.minimum(along_y, 0.0) / 6.0
    zeros = np.zeros_like(forth)
    coefs = np.stack(
        [
            along_x,
            forth,
            -6.0 * forth - 2.0 * back,
            3.0 * forth - 3.0 * back,
            2.0 * forth + 6.0 * back,
            -back,
            zeros,
            zeros,
        ],
        axis=1,
    )
    coefs = lax.dynamic_slice_in_dim(jnp.asarray(coefs, jnp.float32), lax.axis_index("bins") * local_bins, local_bins)
    sea_cells = sea_mask.astype(jnp.float32)
    strip = 0.5 * cell_means(current).T
    strip_cols = strip.shape[1]
    low_side = jnp.swapaxes(spectrum[:, :2, :] * sea_cells[None, :2, :], 0, 1)
    high_side = jnp.swapaxes(spectrum[:, -2:, :] * sea_cells[None, -2:, :], 0, 1)
    low, high = exchange_rows(low_side, high_side)
    strips = gather_strips(jnp.pad(strip, ((0, 0), (0, TILE - strip_cols))), count)
    half = jnp.swapaxes(strips[:, :, :strip_cols], 0, 1).reshape(row_count, col_count)
    ones = jnp.ones((2, col_count), jnp.float32)
    first = transport_call(spectrum, low, high, sea_cells, half, coefs, ones, True)
    middle, low, high, stokes = middle_call(
        first, partner_plus, partner_minus, strength, drift_table, source_map, count, bands
    )
    inside = jnp.stack([band > 0, band < bands - 1]).astype(jnp.float32)
    edges = jnp.broadcast_to(inside[:, None], (2, col_count))
    second = transport_call(middle, low, high, sea_cells, half, coefs, edges, False)
    return (second, stokes.reshape(2, LEV, *source_map.shape))


def on_device(spectrum, sea_mask, current, partner_plus, partner_minus, source_map):
    count = lax.axis_size("bins")
    bins, rows, cols = spectrum.shape
    bands = lax.axis_size("lat")
    lons, lats = source_map.shape
    fits = (
        rows % count == 0
        and rows % 8 == 0
        and bins % 8 == 0
        and cols % TILE == 0
        and cols // count % 8 == 0
        and cols // count <= TILE
        and bins * count % TILE == 0
        and 4 * lats == TILE
        and lats == 2 * rows
        and lons % 8 == 0
        and count > 1
        and bands > 1
    )
    body = on_device_fast if fits else on_device_plain
    return body(spectrum, sea_mask, current, partner_plus, partner_minus, source_map)


def solution(mesh):
    return jax.shard_map(
        on_device,
        mesh=mesh,
        in_specs=(
            P("bins", "lat", None),
            P("lat", None),
            P("bins", "lat"),
            P(),
            P(),
            P("bins", "lat"),
        ),
        out_specs=(P("bins", "lat", None), P(None, None, "bins", "lat")),
        check_vma=False,
    )
```
